256 devices in a mesh: req: 4 (over y), blk: 32 (over z, x), head: 2 (over core).
Axes of the slice: x: 4, y: 4, z: 8, core: 2. Of those that a mesh axis runs over, the one named last changes fastest.
Arguments:
- queries: bfloat16 [65536, 3584], P(('req', 'blk'), 'head'), parts along dimension 0, may hold values from -32 to 32
- keys: bfloat16 [65536, 3584], P(('req', 'blk'), 'head'), parts along dimension 0, may hold values from -32 to 32
- values: bfloat16 [65536, 3584], P(('req', 'blk'), 'head'), parts along dimension 0, may hold values from -6 to 6
- segment_ids: int32 [65536], P(('req', 'blk')), parts along dimension 0, may hold values from 0 to 15, never falling along the last dimension, each value on 1 to 2048 neighbouring positions
- page_table: int32 [512], P(('req', 'blk')), parts along dimension 0, may hold values from 0 to 127, as said below
Outputs:
- attended: bfloat16 [65536, 3584], P(('req', 'blk'), 'head'), parts along dimension 0
- kv_cache: bfloat16 [512, 128, 2, 3584], P(('req', 'blk'), None, None, 'head'), parts along dimension 0
The draws below stay inside these ranges and needn't reach their ends.
There are 4 independent parts, one for each index of `req`. The reference program is written for one: setup_inputs(seed, part) draws one part's arguments, and reference() takes and returns one part's arrays. A program takes and returns all parts, laid end to end along the dimension named above; each array names one. Nothing has to cross between parts.
Inputs may be any that keep to these rules, and one draw needn't show every extreme that they name: segment_ids never fall along the packed tokens and take every value 0 to 15; each prompt holds 1 to 2048 tokens, one exactly 2048. page_table names every cache slot exactly once; the pages of the packed block b (its 512 tokens) take, in a drawn order, the slots of the pages of block b + 4, counted around the group past the last block to the first.
All inputs are finite; a program needn't handle non-finite values.
Results may differ from the reference program's by a relative error of at most 0.0055.
Values may be sent and summed in bfloat16 or wider, within the bound.
No kernel may reach another device: no remote copies, remote signals or barrier semaphores. Data moves between devices by JAX's collectives and lax.ppermute only.
A program may use at most 128 MiB of HBM per device.

```python
import math
import jax
import jax.numpy as jnp
import numpy as np
from jax import lax

TOK_DEV = 512
HEADS = 16
HD = 224
PAGE = 128
REACH = 4
MOST = 2048
NSEG = 16
TOKENS = 16384
PAGES = 128


def query_key_pair(key):
    base = jax.random.fold_in(key, 7)
    key_branch, query_branch = jax.random.split(base, 2)
    shape = (TOKENS, HEADS * HD)
    drawn_keys = jax.random.truncated_normal(key_branch, -6.0, 6.0, shape, jnp.float32)
    drawn_queries = jax.random.truncated_normal(query_branch, -6.0, 6.0, shape, jnp.float32)
    return (drawn_queries, drawn_keys)


def draw_queries(key, part):
    return query_key_pair(key)[0].astype(jnp.bfloat16)


def draw_keys(key, part):
    return query_key_pair(key)[1].astype(jnp.bfloat16)


def draw_page_table(key, part):
    per_block = TOK_DEV // PAGE
    block_count = PAGES // per_block
    order_key = jax.random.fold_in(key, 11)
    ranks = jax.random.randint(order_key, (block_count, per_block), 0, 1 << 20) * per_block + jnp.arange(per_block, dtype=jnp.int32)[None, :]
    order = jnp.argsort(ranks, axis=1, stable=True).astype(jnp.int32)
    owner = (jnp.arange(block_count, dtype=jnp.int32) + REACH) % block_count
    return (owner[:, None] * per_block + order).reshape(PAGES).astype(jnp.int32)


def block_levels(own_key, extent, pieces, smallest, top_value):
    loudness, own = 1.0, jax.random.fold_in(own_key, 6)
    for position, blocks in pieces:
        draws = jnp.exp(jax.random.uniform(jax.random.fold_in(own, position), (blocks,), jnp.float32, smallest / len(pieces), top_value / len(pieces)))
        loudness = loudness * jnp.repeat(draws, extent[position] // blocks).reshape([-1 if axis == position else 1 for axis in range(len(extent))])
    return loudness


def profile(number_of, total, most, lean):
    portions = [(1 << 20) // math.isqrt(standing ** lean) + 1 for standing in range(2, number_of + 1)]
    spare, counts = total - most - (number_of - 1), [1] * (number_of - 1)
    while spare > 0:
        free = [i for i in range(number_of - 1) if counts[i] < most]
        whole, budget = sum([portions[i] for i in free]), spare
        for i in free:
            addition = min(most - counts[i], max(1, budget * portions[i] // whole), spare)
            counts[i] = counts[i] + addition
            spare = spare - addition
    return np.array([most] + counts)


def uneven_parts(stream_key, count, total, most, lean):
    if count == 2:
        one = jax.random.randint(stream_key, (), max(1, total - most), min(most, total - 1) + 1)
        return jnp.stack([one, total - one])
    tallies = jnp.asarray(profile(count, total, most, lean), jnp.int32)
    twos = (count - 1) // 2
    giver, receiver = tallies[1:1 + 2 * twos:2], tallies[2:2 + 2 * twos:2]
    room = jnp.minimum(giver - 1, most - receiver)
    moved = jax.random.randint(jax.random.fold_in(stream_key, 1), (twos,), 0, 1 << 20) % (room + 1)
    tallies = tallies.at[1:1 + 2 * twos:2].set(giver - moved).at[2:2 + 2 * twos:2].set(receiver + moved)
    return tallies[jax.random.permutation(jax.random.fold_in(stream_key, 2), count)]


def gaussian(key, dims, spread, reach, shards=(), kind=jnp.bfloat16):
    values = jax.random.normal(key, dims, jnp.float32) * spread
    if len(shards) > 0:
        values = block_levels(key, dims, shards, -0.22, 0.18) * values
    return jnp.clip(values, min=-reach, max=reach).astype(kind)


def setup_inputs(seed: int = 0, part: int = 0) -> dict:
    key_of = jax.random.split(jax.random.key(seed), 6)
    part_keys = jax.random.split(jax.random.fold_in(key_of[5], part), 6)
    return {
        "queries": draw_queries(jax.random.fold_in(jax.random.fold_in(key_of[5], part), 71), part),
        "keys": draw_keys(jax.random.fold_in(jax.random.fold_in(key_of[5], part), 71), part),
        "values": gaussian(part_keys[2], (TOKENS, HEADS * HD), 1.0, 6.0, ((0, 32), (1, 2))),
        "segment_ids": jnp.searchsorted(jnp.cumsum(uneven_parts(part_keys[3], NSEG, TOKENS, MOST, 2)), jnp.arange(TOKENS), side="right").astype(jnp.int32),
        "page_table": draw_page_table(jax.random.fold_in(jax.random.fold_in(key_of[5], part), 71), part),
    }


NEG = -1e30


def reference(queries, keys, values, segment_ids, page_table):
    tokens = queries.shape[0]
    width = HEADS * HD
    scale = (HD / 2.0) ** -0.5
    query_grid = queries.reshape(tokens, HEADS, HD).astype(jnp.float32)
    key_grid = jnp.concatenate([jnp.zeros((MOST, HEADS, HD), jnp.float32), keys.reshape(tokens, HEADS, HD).astype(jnp.float32)], axis=0)
    value_grid = jnp.concatenate([jnp.zeros((MOST, HEADS, HD), jnp.float32), values.reshape(tokens, HEADS, HD).astype(jnp.float32)], axis=0)
    padded_seg = jnp.concatenate([jnp.full((MOST,), -1, jnp.int32), segment_ids.astype(jnp.int32)], axis=0)
    padded_pos = jnp.arange(tokens + MOST, dtype=jnp.int32) - MOST
    block = math.gcd(tokens, 512)
    window = MOST + block

    def one_block(index):
        start = (index * block).astype(jnp.int32)
        part_q = lax.dynamic_slice_in_dim(query_grid, start, block, 0)
        part_seg = lax.dynamic_slice_in_dim(segment_ids, start, block, 0)
        part_pos = start + jnp.arange(block, dtype=jnp.int32)
        near_keys = lax.dynamic_slice_in_dim(key_grid, start, window, 0)
        near_values = lax.dynamic_slice_in_dim(value_grid, start, window, 0)
        near_seg = lax.dynamic_slice_in_dim(padded_seg, start, window, 0)
        near_pos = lax.dynamic_slice_in_dim(padded_pos, start, window, 0)
        scores = jnp.einsum("thd,uhd->htu", part_q, near_keys) * scale
        allowed = (part_seg[:, None] == near_seg[None, :]) & (near_pos[None, :] <= part_pos[:, None])
        scores = jnp.where(allowed[None], scores, NEG)
        top = jnp.max(scores, axis=2, keepdims=True)
        weights = jnp.where(allowed[None], jnp.exp(scores - top), jnp.float32(0.0))
        total = jnp.sum(weights, axis=2)
        rounded = lax.optimization_barrier(weights.astype(jnp.bfloat16)).astype(jnp.float32)
        mixed = jnp.einsum("htu,uhd->thd", rounded, near_values) / total.T[:, :, None]
        return mixed.reshape(block, width).astype(jnp.bfloat16)

    attended = lax.map(one_block, jnp.arange(tokens // block, dtype=jnp.int32)).reshape(tokens, width)
    pages = jnp.stack([keys, values], axis=1).reshape(PAGES, PAGE, 2, width)
    kv_cache = jnp.zeros_like(pages).at[page_table].set(pages)
    return attended, kv_cache
```

```python
import jax
import jax.numpy as jnp
from jax import lax
from jax.experimental import pallas as pl
from jax.experimental.pallas import tpu as pltpu
from jax.sharding import PartitionSpec as P

HD = 224
PAGE = 128
NSEG = 16
COLS = 4
SLAB = COLS * HD
WIDE = 256
TQ = 256
TK = 512
NEG = -1e30
SCALE_LOG2 = (HD / 2.0) ** (-0.5) * 1.4426950408889634

VMEM = pl.BlockSpec(memory_space=pltpu.VMEM)
SMEM = pl.BlockSpec(memory_space=pltpu.SMEM)


def params():
    return pltpu.CompilerParams(vmem_limit_bytes=48 * 1024 * 1024)


def regroup(parts):
    return [
        jnp.concatenate([part[:, b * HD : (b + 1) * HD] for part in parts], axis=1)
        for b in range(COLS)
    ]


def pack_kernel(col_ref, q_ref, k_ref, v_ref, own, one, two, three, zrow, zlate, held):
    col = col_ref[0]
    outs = (own, one, two, three)
    for t, ref in enumerate((q_ref, k_ref, v_ref)):
        pages = [ref[p * PAGE : (p + 1) * PAGE, :] for p in range(COLS)]
        for j, piece in enumerate(regroup(pages)):
            held[t, j] = piece
    for r in range(COLS):
        slot = lax.rem(col + r, COLS)
        for t in range(3):
            outs[r][t] = held[t, slot]
        for t in range(2):
            if r == 2:
                zlate[t] = held[t + 1, slot]
            else:
                zrow[(0, 1, None, 2)[r], t] = held[t + 1, slot]


def pack(col, queries, keys, values, half):
    block = pl.BlockSpec((COLS * PAGE, SLAB), lambda i: (0, half))
    piece = jax.ShapeDtypeStruct((3, PAGE, SLAB), jnp.bfloat16)
    return pl.pallas_call(
        pack_kernel,
        grid=(1,),
        out_shape=[piece] * 4
        + [
            jax.ShapeDtypeStruct((3, 2, PAGE, SLAB), jnp.bfloat16),
            jax.ShapeDtypeStruct((2, PAGE, SLAB), jnp.bfloat16),
        ],
        in_specs=[SMEM, block, block, block],
        out_specs=[VMEM] * 6,
        scratch_shapes=[pltpu.VMEM((3, COLS, PAGE, SLAB), jnp.bfloat16)],
        compiler_params=params(),
        name="pack",
        cost_estimate=pl.CostEstimate(flops=0, transcendentals=0, bytes_accessed=6 * 1024 * 1024),
    )(col, queries, keys, values)


def attend_kernel(
    col_ref, start_smem, start_ref, a0, a1, a2, a3, zrow, p1, p2, p3,
    o0, o1, o2, o3, qs, ks, vs, os, m_ref, acc_ref,
):
    col = col_ref[0]
    rows = COLS * PAGE
    zeros = jnp.zeros((PAGE, WIDE - HD), jnp.bfloat16)
    ones = jnp.ones((PAGE, WIDE - HD), jnp.bfloat16)

    def spread(dst, base, piece, fill):
        for p in range(COLS):
            at = pl.multiple_of(base + p * PAGE, PAGE)
            dst[pl.ds(at, PAGE), :] = jnp.concatenate(
                [piece[:, p * HD : (p + 1) * HD], fill], axis=1
            )

    for r, ref in enumerate((a0, a1, a2, a3)):
        base = lax.rem(col - r + COLS, COLS) * rows
        spread(qs, base, ref[0], zeros)
        spread(ks, base + COLS * rows, ref[1], zeros)
        spread(vs, base + COLS * rows, ref[2], ones)
    for r, ref in enumerate((zrow.at[0], p1, p2, p3)):
        base = lax.rem(col - r + COLS, COLS) * rows
        spread(ks, base, ref[0], zeros)
        spread(vs, base, ref[1], ones)

    per = rows // TQ

    def query_tile(i, _):
        c = lax.div(i, per)
        r = lax.rem(col - c + COLS, COLS)
        off = pl.multiple_of(lax.rem(i, per) * TQ, TQ)
        qb = pl.multiple_of(i * TQ, TQ)
        t0 = COLS * rows + qb
        s_first = start_smem[r * rows + off]
        s_last = start_smem[r * rows + off + TQ - 1]
        m_ref[...] = jnp.full_like(m_ref, NEG)
        acc_ref[...] = jnp.zeros_like(acc_ref)

        def tile(kb, masked):
            s = lax.dot_general(
                qs[pl.ds(qb, TQ), :], ks[pl.ds(kb, TK), :],
                (((1,), (1,)), ((), ())), preferred_element_type=jnp.float32,
            )
            if masked:
                u = kb + lax.broadcasted_iota(jnp.int32, (TQ, TK), 1)
                t = t0 + lax.broadcasted_iota(jnp.int32, (TQ, TK), 0)
                first = jnp.tile(start_ref[r, pl.ds(off, TQ), :], (1, TK // 128))
                s = jnp.where((u >= first) & (u <= t), s, NEG)
            m_old = m_ref[...]
            m_new = jnp.maximum(m_old, jnp.max(s, axis=1, keepdims=True))
            m_ref[...] = m_new
            fade = jnp.exp2((m_old - m_new) * SCALE_LOG2)
            w = jnp.exp2((s - jnp.tile(m_new, (1, TK // 128))) * SCALE_LOG2)
            acc_ref[...] = acc_ref[...] * jnp.tile(fade, (1, WIDE // 128)) + jnp.dot(
                w.astype(jnp.bfloat16), vs[pl.ds(kb, TK), :], preferred_element_type=jnp.float32
            )

        def key_tile(kk, _):
            kb = pl.multiple_of(kk * TK, TK)
            full = (kb >= s_last) & (kb + TK - 1 <= t0)

            @pl.when(full)
            def _():
                tile(kb, False)

            @pl.when(jnp.logical_not(full))
            def _():
                tile(kb, True)

            return 0

        lax.fori_loop(lax.div(s_first, TK), lax.div(t0 + TQ - 1, TK) + 1, key_tile, 0)
        total = acc_ref[...]
        os[pl.ds(qb, TQ), :] = (total / total[:, HD : HD + 1]).astype(jnp.bfloat16)
        return 0

    lax.fori_loop(0, COLS * per, query_tile, 0)
    for r, out in enumerate((o0, o1, o2, o3)):
        base = lax.rem(col + r, COLS) * rows
        out[...] = jnp.concatenate(
            [os[pl.ds(pl.multiple_of(base + p * PAGE, PAGE), PAGE), :][:, :HD] for p in range(COLS)],
            axis=1,
        )


def attend(col, start_flat, start_wide, own, zrow, prior):
    rows = COLS * PAGE
    total = COLS * rows
    piece = jax.ShapeDtypeStruct((PAGE, SLAB), jnp.bfloat16)
    return pl.pallas_call(
        attend_kernel,
        out_shape=[piece] * 4,
        in_specs=[SMEM, SMEM] + [VMEM] * 9,
        out_specs=[VMEM] * 4,
        scratch_shapes=[
            pltpu.VMEM((total, WIDE), jnp.bfloat16),
            pltpu.VMEM((2 * total, WIDE), jnp.bfloat16),
            pltpu.VMEM((2 * total, WIDE), jnp.bfloat16),
            pltpu.VMEM((total, WIDE), jnp.bfloat16),
            pltpu.VMEM((TQ, 128), jnp.float32),
            pltpu.VMEM((TQ, WIDE), jnp.float32),
        ],
        compiler_params=params(),
        name="attend",
        cost_estimate=pl.CostEstimate(
            flops=4 * total * total * WIDE, transcendentals=total * total, bytes_accessed=6 * 1024 * 1024
        ),
    )(col, start_flat, start_wide, *own, zrow, *prior)


def unpack_kernel(col_ref, *refs):
    col = col_ref[0]
    out, held = refs[8], refs[9]
    for half in range(2):
        for r in range(COLS):
            held[half, lax.rem(col - r + COLS, COLS)] = refs[half * COLS + r][...]
        parts = [held[half, j] for j in range(COLS)]
        for p, page in enumerate(regroup(parts)):
            out[p * PAGE : (p + 1) * PAGE, half * SLAB : (half + 1) * SLAB] = page


def unpack(col, pieces):
    return pl.pallas_call(
        unpack_kernel,
        out_shape=jax.ShapeDtypeStruct((COLS * PAGE, 2 * SLAB), jnp.bfloat16),
        in_specs=[SMEM] + [VMEM] * 8,
        out_specs=VMEM,
        scratch_shapes=[pltpu.VMEM((2, COLS, PAGE, SLAB), jnp.bfloat16)],
        compiler_params=params(),
        name="unpack",
        cost_estimate=pl.CostEstimate(flops=0, transcendentals=0, bytes_accessed=4 * 1024 * 1024),
    )(col, *pieces)


def cache_kernel(col_ref, slot_ref, zrow_a, zlate_a, zrow_b, zlate_b, out, held):
    col = col_ref[0]
    for half, (zrow, zlate) in enumerate(((zrow_a, zlate_a), (zrow_b, zlate_b))):
        for r in range(COLS):
            at = lax.rem(col + r, COLS)
            for t in range(2):
                held[t, at] = zlate[t] if r == 2 else zrow[(0, 1, None, 2)[r], t]
        for t in range(2):
            parts = [held[t, j] for j in range(COLS)]
            for p, page in enumerate(regroup(parts)):
                out[slot_ref[p], :, t, half * SLAB : (half + 1) * SLAB] = page


def cache(col, slots, zrow_a, zlate_a, zrow_b, zlate_b):
    return pl.pallas_call(
        cache_kernel,
        out_shape=jax.ShapeDtypeStruct((COLS, PAGE, 2, 2 * SLAB), jnp.bfloat16),
        in_specs=[SMEM, SMEM] + [VMEM] * 4,
        out_specs=VMEM,
        scratch_shapes=[pltpu.VMEM((2, COLS, PAGE, SLAB), jnp.bfloat16)],
        compiler_params=params(),
        name="cache",
        cost_estimate=pl.CostEstimate(flops=0, transcendentals=0, bytes_accessed=8 * 1024 * 1024),
    )(col, slots, zrow_a, zlate_a, zrow_b, zlate_b)


def per_device(queries, keys, values, segment_ids, page_table):
    blocks = lax.axis_size("blk")
    index = lax.axis_index("blk")
    col = lax.rem(index, COLS).astype(jnp.int32).reshape(1)
    count = queries.shape[0]
    pages = page_table.shape[0]

    def across(value, r):
        route = [(i, i - i % COLS + (i % COLS + r) % COLS) for i in range(blocks)]
        return lax.ppermute(value, "blk", route)

    def ahead(value):
        return lax.ppermute(value, "blk", [(i, (i + COLS) % blocks) for i in range(blocks)])

    row_seg = jnp.stack([segment_ids] + [across(segment_ids, r) for r in (1, 2, 3)])
    slots_here = jnp.broadcast_to(page_table[:, None], (pages, count // pages)).reshape(1, count)
    got = ahead(jnp.concatenate([row_seg, slots_here]))
    prior_seg = jnp.where(index < COLS, -1, got[:COLS])
    slots = got[COLS, :: count // pages] - index * pages
    numbers = jnp.arange(NSEG, dtype=jnp.int32)
    below = jnp.sum(
        (row_seg[None] < numbers[:, None, None]).astype(jnp.int32)
        + (prior_seg[None] < numbers[:, None, None]).astype(jnp.int32),
        axis=(1, 2),
    )
    start = jnp.sum(jnp.where(row_seg[..., None] == numbers, below, 0), axis=-1)
    start_flat = start.reshape(COLS * count)
    start_wide = jnp.broadcast_to(start[..., None], (COLS, count, 128))

    packed = [pack(col, queries, keys, values, half) for half in range(2)]
    row, zrow, zlate, prior = [], [], [], []
    for own, one, two, three, z_now, z_late in packed:
        row.append((own, across(one, 1), across(two, 2), across(three, 3)))
        zrow.append(ahead(z_now))
    for half in range(2):
        passed = ahead(row[half][2][1:])
        prior.append((across(zrow[half][1], 1), passed, across(zrow[half][2], 3)))
    for half in range(2):
        zlate.append(ahead(packed[half][5]))
    pieces = []
    for half in range(2):
        o0, o1, o2, o3 = attend(col, start_flat, start_wide, row[half], zrow[half], prior[half])
        pieces += [o0, across(o1, 1), across(o2, 2), across(o3, 3)]
    mixed = unpack(col, pieces)
    kv = cache(col, slots, zrow[0], zlate[0], zrow[1], zlate[1])
    return (mixed, kv)


def solution(mesh):
    in_specs = (
        P(("req", "blk"), "head"),
        P(("req", "blk"), "head"),
        P(("req", "blk"), "head"),
        P(("req", "blk")),
        P(("req", "blk")),
    )
    out_specs = (P(("req", "blk"), "head"), P(("req", "blk"), None, None, "head"))
    return jax.shard_map(
        per_device, mesh=mesh, in_specs=in_specs, out_specs=out_specs, check_vma=False
    )
```

```python
import jax
import jax.numpy as jnp
from jax import lax
from jax.experimental import pallas as pl
from jax.experimental.pallas import tpu as pltpu
from jax.sharding import PartitionSpec as P

HD = 224
PAGE = 128
NSEG = 16
COLS = 4
SLAB = COLS * HD
WIDE = 256
TQ = 256
TK = 512
NEG = -1e30
SCALE_LOG2 = (HD / 2.0) ** (-0.5) * 1.4426950408889634

VMEM = pl.BlockSpec(memory_space=pltpu.VMEM)
SMEM = pl.BlockSpec(memory_space=pltpu.SMEM)


def params():
    return pltpu.CompilerParams(vmem_limit_bytes=48 * 1024 * 1024)


def regroup(parts):
    return [
        jnp.concatenate([part[:, b * HD : (b + 1) * HD] for part in parts], axis=1)
        for b in range(COLS)
    ]


def pack_kernel(col_ref, q_ref, k_ref, v_ref, *refs):
    own, one, two, three, zrow, zlate, held = refs[-7:]
    col = col_ref[0]
    outs = (own, one, two, three)
    for t, ref in enumerate((q_ref, k_ref, v_ref)):
        pages = [ref[p * PAGE : (p + 1) * PAGE, :] for p in range(COLS)]
        for j, piece in enumerate(regroup(pages)):
            held[t, j] = piece
    for r in range(COLS):
        slot = lax.rem(col + r, COLS)
        for t in range(3):
            outs[r][t] = held[t, slot]
        for t in range(2):
            if r == 2:
                zlate[t] = held[t + 1, slot]
            else:
                zrow[(0, 1, None, 2)[r], t] = held[t + 1, slot]


def pack(col, queries, keys, values, half, after):
    block = pl.BlockSpec((COLS * PAGE, SLAB), lambda i: (0, half))
    piece = jax.ShapeDtypeStruct((3, PAGE, SLAB), jnp.bfloat16)
    return pl.pallas_call(
        pack_kernel,
        grid=(1,),
        out_shape=[piece] * 4
        + [
            jax.ShapeDtypeStruct((3, 2, PAGE, SLAB), jnp.bfloat16),
            jax.ShapeDtypeStruct((2, PAGE, SLAB), jnp.bfloat16),
        ],
        in_specs=[SMEM, block, block, block] + [pl.BlockSpec(memory_space=pl.ANY)] * len(after),
        out_specs=[VMEM] * 6,
        scratch_shapes=[pltpu.VMEM((3, COLS, PAGE, SLAB), jnp.bfloat16)],
        compiler_params=params(),
        name="pack",
        cost_estimate=pl.CostEstimate(flops=0, transcendentals=0, bytes_accessed=6 * 1024 * 1024),
    )(col, queries, keys, values, *after)


def attend_kernel(
    col_ref, start_smem, start_ref, a0, a1, a2, a3, zrow, p1, p2, p3,
    o0, o1, o2, o3, qs, ks, vs, os, m_ref, acc_ref,
):
    col = col_ref[0]
    rows = COLS * PAGE
    zeros = jnp.zeros((PAGE, WIDE - HD), jnp.bfloat16)
    ones = jnp.ones((PAGE, WIDE - HD), jnp.bfloat16)

    def spread(dst, base, piece, fill):
        for p in range(COLS):
            at = pl.multiple_of(base + p * PAGE, PAGE)
            dst[pl.ds(at, PAGE), :] = jnp.concatenate(
                [piece[:, p * HD : (p + 1) * HD], fill], axis=1
            )

    for r, ref in enumerate((a0, a1, a2, a3)):
        base = lax.rem(col - r + COLS, COLS) * rows
        spread(qs, base, ref[0], zeros)
        spread(ks, base + COLS * rows, ref[1], zeros)
        spread(vs, base + COLS * rows, ref[2], ones)
    for r, ref in enumerate((zrow.at[0], p1, p2, p3)):
        base = lax.rem(col - r + COLS, COLS) * rows
        spread(ks, base, ref[0], zeros)
        spread(vs, base, ref[1], ones)

    per = rows // TQ

    def query_tile(i, _):
        c = lax.div(i, per)
        r = lax.rem(col - c + COLS, COLS)
        off = pl.multiple_of(lax.rem(i, per) * TQ, TQ)
        qb = pl.multiple_of(i * TQ, TQ)
        t0 = COLS * rows + qb
        s_first = start_smem[r * rows + off]
        s_last = start_smem[r * rows + off + TQ - 1]
        m_ref[...] = jnp.full_like(m_ref, NEG)
        acc_ref[...] = jnp.zeros_like(acc_ref)

        def tile(kb, masked):
            s = lax.dot_general(
                qs[pl.ds(qb, TQ), :], ks[pl.ds(kb, TK), :],
                (((1,), (1,)), ((), ())), preferred_element_type=jnp.float32,
            )
            if masked:
                u = kb + lax.broadcasted_iota(jnp.int32, (TQ, TK), 1)
                t = t0 + lax.broadcasted_iota(jnp.int32, (TQ, TK), 0)
                first = jnp.tile(start_ref[r, pl.ds(off, TQ), :], (1, TK // 128))
                s = jnp.where((u >= first) & (u <= t), s, NEG)
            m_old = m_ref[...]
            m_new = jnp.maximum(m_old, jnp.max(s, axis=1, keepdims=True))
            m_ref[...] = m_new
            fade = jnp.exp2((m_old - m_new) * SCALE_LOG2)
            w = jnp.exp2((s - jnp.tile(m_new, (1, TK // 128))) * SCALE_LOG2)
            acc_ref[...] = acc_ref[...] * jnp.tile(fade, (1, WIDE // 128)) + jnp.dot(
                w.astype(jnp.bfloat16), vs[pl.ds(kb, TK), :], preferred_element_type=jnp.float32
            )

        def key_tile(kk, _):
            kb = pl.multiple_of(kk * TK, TK)
            full = (kb >= s_last) & (kb + TK - 1 <= t0)

            @pl.when(full)
            def _():
                tile(kb, False)

            @pl.when(jnp.logical_not(full))
            def _():
                tile(kb, True)

            return 0

        lax.fori_loop(lax.div(s_first, TK), lax.div(t0 + TQ - 1, TK) + 1, key_tile, 0)
        total = acc_ref[...]
        os[pl.ds(qb, TQ), :] = (total / total[:, HD : HD + 1]).astype(jnp.bfloat16)
        return 0

    lax.fori_loop(0, COLS * per, query_tile, 0)
    for r, out in enumerate((o0, o1, o2, o3)):
        base = lax.rem(col + r, COLS) * rows
        out[...] = jnp.concatenate(
            [os[pl.ds(pl.multiple_of(base + p * PAGE, PAGE), PAGE), :][:, :HD] for p in range(COLS)],
            axis=1,
        )


def attend(col, start_flat, start_wide, own, zrow, prior):
    rows = COLS * PAGE
    total = COLS * rows
    piece = jax.ShapeDtypeStruct((PAGE, SLAB), jnp.bfloat16)
    return pl.pallas_call(
        attend_kernel,
        out_shape=[piece] * 4,
        in_specs=[SMEM, SMEM] + [VMEM] * 9,
        out_specs=[VMEM] * 4,
        scratch_shapes=[
            pltpu.VMEM((total, WIDE), jnp.bfloat16),
            pltpu.VMEM((2 * total, WIDE), jnp.bfloat16),
            pltpu.VMEM((2 * total, WIDE), jnp.bfloat16),
            pltpu.VMEM((total, WIDE), jnp.bfloat16),
            pltpu.VMEM((TQ, 128), jnp.float32),
            pltpu.VMEM((TQ, WIDE), jnp.float32),
        ],
        compiler_params=params(),
        name="attend",
        cost_estimate=pl.CostEstimate(
            flops=4 * total * total * WIDE, transcendentals=total * total, bytes_accessed=6 * 1024 * 1024
        ),
    )(col, start_flat, start_wide, *own, zrow, *prior)


def unpack_kernel(col_ref, *refs):
    col = col_ref[0]
    out, held = refs[8], refs[9]
    for half in range(2):
        for r in range(COLS):
            held[half, lax.rem(col - r + COLS, COLS)] = refs[half * COLS + r][...]
        parts = [held[half, j] for j in range(COLS)]
        for p, page in enumerate(regroup(parts)):
            out[p * PAGE : (p + 1) * PAGE, half * SLAB : (half + 1) * SLAB] = page


def unpack(col, pieces):
    return pl.pallas_call(
        unpack_kernel,
        out_shape=jax.ShapeDtypeStruct((COLS * PAGE, 2 * SLAB), jnp.bfloat16),
        in_specs=[SMEM] + [VMEM] * 8,
        out_specs=VMEM,
        scratch_shapes=[pltpu.VMEM((2, COLS, PAGE, SLAB), jnp.bfloat16)],
        compiler_params=params(),
        name="unpack",
        cost_estimate=pl.CostEstimate(flops=0, transcendentals=0, bytes_accessed=4 * 1024 * 1024),
    )(col, *pieces)


def cache_kernel(col_ref, slot_ref, zrow_a, zlate_a, zrow_b, zlate_b, out, held):
    col = col_ref[0]
    for half, (zrow, zlate) in enumerate(((zrow_a, zlate_a), (zrow_b, zlate_b))):
        for r in range(COLS):
            at = lax.rem(col + r, COLS)
            for t in range(2):
                held[t, at] = zlate[t] if r == 2 else zrow[(0, 1, None, 2)[r], t]
        for t in range(2):
            parts = [held[t, j] for j in range(COLS)]
            for p, page in enumerate(regroup(parts)):
                out[slot_ref[p], :, t, half * SLAB : (half + 1) * SLAB] = page


def cache(col, slots, zrow_a, zlate_a, zrow_b, zlate_b):
    return pl.pallas_call(
        cache_kernel,
        out_shape=jax.ShapeDtypeStruct((COLS, PAGE, 2, 2 * SLAB), jnp.bfloat16),
        in_specs=[SMEM, SMEM] + [VMEM] * 4,
        out_specs=VMEM,
        scratch_shapes=[pltpu.VMEM((2, COLS, PAGE, SLAB), jnp.bfloat16)],
        compiler_params=params(),
        name="cache",
        cost_estimate=pl.CostEstimate(flops=0, transcendentals=0, bytes_accessed=8 * 1024 * 1024),
    )(col, slots, zrow_a, zlate_a, zrow_b, zlate_b)


def per_device(queries, keys, values, segment_ids, page_table):
    blocks = lax.axis_size("blk")
    index = lax.axis_index("blk")
    col = lax.rem(index, COLS).astype(jnp.int32).reshape(1)
    count = queries.shape[0]
    pages = page_table.shape[0]

    def across(value, r):
        route = [(i, i - i % COLS + (i % COLS + r) % COLS) for i in range(blocks)]
        return lax.ppermute(value, "blk", route)

    def ahead(value):
        return lax.ppermute(value, "blk", [(i, (i + COLS) % blocks) for i in range(blocks)])

    def behind(value, *done):
        return lax.optimization_barrier((value, *done))[0]

    numbers = jnp.arange(NSEG, dtype=jnp.int32)
    below = jnp.sum((segment_ids < numbers[:, None]).astype(jnp.int32), axis=1)
    named = lax.dynamic_update_slice(
        jnp.zeros((blocks * pages,), jnp.int32), page_table, (index * pages,)
    )
    shared = lax.psum(jnp.concatenate([below, named]), "blk")
    source = lax.rem(index + blocks - COLS, blocks)
    slots = lax.dynamic_slice(shared, (NSEG + source * pages,), (pages,)) - index * pages
    width = COLS * count
    at = COLS * count - lax.div(index, COLS) * width
    home = jnp.stack([lax.rem(col[0] - r + COLS, COLS) for r in range(COLS)])
    here = width + home[:, None] * count + jnp.arange(count, dtype=jnp.int32)
    begin = shared[:NSEG] + at
    start = jnp.max(
        jnp.where(begin <= here[..., None], begin, -(2**30)), axis=-1
    ).astype(jnp.int32)
    start_flat = start.reshape(width)
    start_wide = jnp.broadcast_to(start[..., None], (COLS, count, 128))

    pieces, late, zrows, wait, attended = [], [], [], (), None
    for half in range(2):
        own, one, two, three, z_now, z_late = pack(col, queries, keys, values, half, wait)
        zrow = ahead(z_now)
        row = (own, across(one, 1), across(two, 2), across(three, 3))
        wait = (zrow, row[2])
        from_z1, from_row, from_z3 = zrow[1], row[2][1:], zrow[2]
        if attended is not None:
            from_z1, from_row, from_z3 = (behind(x, attended) for x in (from_z1, from_row, from_z3))
        prior = (across(from_z1, 1), ahead(from_row), across(from_z3, 3))
        outs = attend(col, start_flat, start_wide, row, zrow, prior)
        attended = outs[0]
        pieces += [outs[0]] + [across(outs[r], r) for r in (1, 2, 3)]
        late.append(z_late)
        zrows.append(zrow)
    late = [ahead(behind(x, zrows[1])) for x in late]
    mixed = unpack(col, pieces)
    kv = cache(col, slots, zrows[0], late[0], zrows[1], late[1])
    return (mixed, kv)


def solution(mesh):
    in_specs = (
        P(("req", "blk"), "head"),
        P(("req", "blk"), "head"),
        P(("req", "blk"), "head"),
        P(("req", "blk")),
        P(("req", "blk")),
    )
    out_specs = (P(("req", "blk"), "head"), P(("req", "blk"), None, None, "head"))
    return jax.shard_map(
        per_device, mesh=mesh, in_specs=in_specs, out_specs=out_specs, check_vma=False
    )
```

```python
import jax
import jax.numpy as jnp
from jax import lax
from jax.experimental import pallas as pl
from jax.experimental.pallas import tpu as pltpu
from jax.sharding import PartitionSpec as P

HD = 224
PAGE = 128
NSEG = 16
COLS = 4
SLAB = COLS * HD
WIDE = 256
TQ = 256
TK = 512
NEG = -1e30
SCALE_LOG2 = (HD / 2.0) ** (-0.5) * 1.4426950408889634

VMEM = pl.BlockSpec(memory_space=pltpu.VMEM)
SMEM = pl.BlockSpec(memory_space=pltpu.SMEM)


def params():
    return pltpu.CompilerParams(vmem_limit_bytes=48 * 1024 * 1024)


def regroup(parts):
    return [
        jnp.concatenate([part[:, b * HD : (b + 1) * HD] for part in parts], axis=1)
        for b in range(COLS)
    ]


def pack_kernel(col_ref, q_ref, k_ref, v_ref, own, one, two, three, zrow, zlate, held):
    col = col_ref[0]
    outs = (own, one, two, three)
    for t, ref in enumerate((q_ref, k_ref, v_ref)):
        pages = [ref[p * PAGE : (p + 1) * PAGE, :] for p in range(COLS)]
        for j, piece in enumerate(regroup(pages)):
            held[t, j] = piece
    for r in range(COLS):
        slot = lax.rem(col + r, COLS)
        for t in range(3):
            outs[r][t] = held[t, slot]
        for t in range(2):
            if r == 2:
                zlate[t] = held[t + 1, slot]
            else:
                zrow[(0, 1, None, 2)[r], t] = held[t + 1, slot]


def pack(col, queries, keys, values, half):
    block = pl.BlockSpec((COLS * PAGE, SLAB), lambda i: (0, half))
    piece = jax.ShapeDtypeStruct((3, PAGE, SLAB), jnp.bfloat16)
    return pl.pallas_call(
        pack_kernel,
        grid=(1,),
        out_shape=[piece] * 4
        + [
            jax.ShapeDtypeStruct((3, 2, PAGE, SLAB), jnp.bfloat16),
            jax.ShapeDtypeStruct((2, PAGE, SLAB), jnp.bfloat16),
        ],
        in_specs=[SMEM, block, block, block],
        out_specs=[VMEM] * 6,
        scratch_shapes=[pltpu.VMEM((3, COLS, PAGE, SLAB), jnp.bfloat16)],
        compiler_params=params(),
        name="pack",
        cost_estimate=pl.CostEstimate(flops=0, transcendentals=0, bytes_accessed=6 * 1024 * 1024),
    )(col, queries, keys, values)


def attend_kernel(
    col_ref, start_smem, start_ref, a0, a1, a2, a3, zrow, p1, p2, p3,
    o0, o1, o2, o3, qs, ks, vs, os, m_ref, acc_ref,
):
    col = col_ref[0]
    rows = COLS * PAGE
    zeros = jnp.zeros((PAGE, WIDE - HD), jnp.bfloat16)
    ones = jnp.ones((PAGE, WIDE - HD), jnp.bfloat16)

    def spread(dst, base, piece, fill):
        for p in range(COLS):
            at = pl.multiple_of(base + p * PAGE, PAGE)
            dst[pl.ds(at, PAGE), :] = jnp.concatenate(
                [piece[:, p * HD : (p + 1) * HD], fill], axis=1
            )

    for r, ref in enumerate((a0, a1, a2, a3)):
        base = lax.rem(col - r + COLS, COLS) * rows
        spread(qs, base, ref[0], zeros)
        spread(ks, base + COLS * rows, ref[1], zeros)
        spread(vs, base + COLS * rows, ref[2], ones)
    for r, ref in enumerate((zrow.at[0], p1, p2, p3)):
        base = lax.rem(col - r + COLS, COLS) * rows
        spread(ks, base, ref[0], zeros)
        spread(vs, base, ref[1], ones)

    per = rows // TQ

    def query_tile(i, _):
        c = lax.div(i, per)
        r = lax.rem(col - c + COLS, COLS)
        off = pl.multiple_of(lax.rem(i, per) * TQ, TQ)
        qb = pl.multiple_of(i * TQ, TQ)
        t0 = COLS * rows + qb
        s_first = start_smem[r * rows + off]
        s_last = start_smem[r * rows + off + TQ - 1]
        m_ref[...] = jnp.full_like(m_ref, NEG)
        acc_ref[...] = jnp.zeros_like(acc_ref)

        def tile(kb, masked):
            s = lax.dot_general(
                qs[pl.ds(qb, TQ), :], ks[pl.ds(kb, TK), :],
                (((1,), (1,)), ((), ())), preferred_element_type=jnp.float32,
            )
            if masked:
                u = kb + lax.broadcasted_iota(jnp.int32, (TQ, TK), 1)
                t = t0 + lax.broadcasted_iota(jnp.int32, (TQ, TK), 0)
                first = jnp.tile(start_ref[r, pl.ds(off, TQ), :], (1, TK // 128))
                s = jnp.where((u >= first) & (u <= t), s, NEG)
            m_old = m_ref[...]
            m_new = jnp.maximum(m_old, jnp.max(s, axis=1, keepdims=True))
            m_ref[...] = m_new
            fade = jnp.exp2((m_old - m_new) * SCALE_LOG2)
            w = jnp.exp2((s - jnp.tile(m_new, (1, TK // 128))) * SCALE_LOG2)
            acc_ref[...] = acc_ref[...] * jnp.tile(fade, (1, WIDE // 128)) + jnp.dot(
                w.astype(jnp.bfloat16), vs[pl.ds(kb, TK), :], preferred_element_type=jnp.float32
            )

        def key_tile(kk, _):
            kb = pl.multiple_of(kk * TK, TK)
            full = (kb >= s_last) & (kb + TK - 1 <= t0)

            @pl.when(full)
            def _():
                tile(kb, False)

            @pl.when(jnp.logical_not(full))
            def _():
                tile(kb, True)

            return 0

        lax.fori_loop(lax.div(s_first, TK), lax.div(t0 + TQ - 1, TK) + 1, key_tile, 0)
        total = acc_ref[...]
        os[pl.ds(qb, TQ), :] = (total / total[:, HD : HD + 1]).astype(jnp.bfloat16)
        return 0

    lax.fori_loop(0, COLS * per, query_tile, 0)
    for r, out in enumerate((o0, o1, o2, o3)):
        base = lax.rem(col + r, COLS) * rows
        out[...] = jnp.concatenate(
            [os[pl.ds(pl.multiple_of(base + p * PAGE, PAGE), PAGE), :][:, :HD] for p in range(COLS)],
            axis=1,
        )


def attend(col, start_flat, start_wide, own, zrow, prior):
    rows = COLS * PAGE
    total = COLS * rows
    piece = jax.ShapeDtypeStruct((PAGE, SLAB), jnp.bfloat16)
    return pl.pallas_call(
        attend_kernel,
        out_shape=[piece] * 4,
        in_specs=[SMEM, SMEM] + [VMEM] * 9,
        out_specs=[VMEM] * 4,
        scratch_shapes=[
            pltpu.VMEM((total, WIDE), jnp.bfloat16),
            pltpu.VMEM((2 * total, WIDE), jnp.bfloat16),
            pltpu.VMEM((2 * total, WIDE), jnp.bfloat16),
            pltpu.VMEM((total, WIDE), jnp.bfloat16),
            pltpu.VMEM((TQ, 128), jnp.float32),
            pltpu.VMEM((TQ, WIDE), jnp.float32),
        ],
        compiler_params=params(),
        name="attend",
        cost_estimate=pl.CostEstimate(
            flops=4 * total * total * WIDE, transcendentals=total * total, bytes_accessed=6 * 1024 * 1024
        ),
    )(col, start_flat, start_wide, *own, zrow, *prior)


def unpack_kernel(col_ref, *refs):
    col = col_ref[0]
    out, held = refs[8], refs[9]
    for half in range(2):
        for r in range(COLS):
            held[half, lax.rem(col - r + COLS, COLS)] = refs[half * COLS + r][...]
        parts = [held[half, j] for j in range(COLS)]
        for p, page in enumerate(regroup(parts)):
            out[p * PAGE : (p + 1) * PAGE, half * SLAB : (half + 1) * SLAB] = page


def unpack(col, pieces):
    return pl.pallas_call(
        unpack_kernel,
        out_shape=jax.ShapeDtypeStruct((COLS * PAGE, 2 * SLAB), jnp.bfloat16),
        in_specs=[SMEM] + [VMEM] * 8,
        out_specs=VMEM,
        scratch_shapes=[pltpu.VMEM((2, COLS, PAGE, SLAB), jnp.bfloat16)],
        compiler_params=params(),
        name="unpack",
        cost_estimate=pl.CostEstimate(flops=0, transcendentals=0, bytes_accessed=4 * 1024 * 1024),
    )(col, *pieces)


def cache_kernel(col_ref, slot_ref, zrow_a, zlate_a, zrow_b, zlate_b, out, held):
    col = col_ref[0]
    for half, (zrow, zlate) in enumerate(((zrow_a, zlate_a), (zrow_b, zlate_b))):
        for r in range(COLS):
            at = lax.rem(col + r, COLS)
            for t in range(2):
                held[t, at] = zlate[t] if r == 2 else zrow[(0, 1, None, 2)[r], t]
        for t in range(2):
            parts = [held[t, j] for j in range(COLS)]
            for p, page in enumerate(regroup(parts)):
                out[slot_ref[p], :, t, half * SLAB : (half + 1) * SLAB] = page


def cache(col, slots, zrow_a, zlate_a, zrow_b, zlate_b):
    return pl.pallas_call(
        cache_kernel,
        out_shape=jax.ShapeDtypeStruct((COLS, PAGE, 2, 2 * SLAB), jnp.bfloat16),
        in_specs=[SMEM, SMEM] + [VMEM] * 4,
        out_specs=VMEM,
        scratch_shapes=[pltpu.VMEM((2, COLS, PAGE, SLAB), jnp.bfloat16)],
        compiler_params=params(),
        name="cache",
        cost_estimate=pl.CostEstimate(flops=0, transcendentals=0, bytes_accessed=8 * 1024 * 1024),
    )(col, slots, zrow_a, zlate_a, zrow_b, zlate_b)


def per_device(queries, keys, values, segment_ids, page_table):
    blocks = lax.axis_size("blk")
    index = lax.axis_index("blk")
    col = lax.rem(index, COLS).astype(jnp.int32).reshape(1)
    count = queries.shape[0]
    pages = page_table.shape[0]

    def across(value, r):
        route = [(i, i - i % COLS + (i % COLS + r) % COLS) for i in range(blocks)]
        return lax.ppermute(value, "blk", route)

    def ahead(value):
        return lax.ppermute(value, "blk", [(i, (i + COLS) % blocks) for i in range(blocks)])

    def behind(value, *done):
        return lax.optimization_barrier((value, *done))[0]

    row_seg = jnp.stack([segment_ids] + [across(segment_ids, r) for r in (1, 2, 3)])
    slots_here = jnp.broadcast_to(page_table[:, None], (pages, count // pages)).reshape(1, count)
    got = ahead(jnp.concatenate([row_seg, slots_here]))
    prior_seg = jnp.where(index < COLS, -1, got[:COLS])
    slots = got[COLS, :: count // pages] - index * pages
    numbers = jnp.arange(NSEG, dtype=jnp.int32)
    below = jnp.sum(
        (row_seg[None] < numbers[:, None, None]).astype(jnp.int32)
        + (prior_seg[None] < numbers[:, None, None]).astype(jnp.int32),
        axis=(1, 2),
    )
    start = jnp.sum(jnp.where(row_seg[..., None] == numbers, below, 0), axis=-1)
    start_flat = start.reshape(COLS * count)
    start_wide = jnp.broadcast_to(start[..., None], (COLS, count, 128))

    packed = [pack(col, queries, keys, values, half) for half in range(2)]
    pieces, late, zrows = [], [], []
    first, turn = got, ()
    attended = None
    for own, one, two, three, z_now, z_late in packed:
        zrow = ahead(behind(z_now, first))
        if turn:
            one, three = behind(one, *turn), behind(three, *turn)
            two = behind(two, first)
        row = (own, across(one, 1), across(two, 2), across(three, 3))
        zrow = behind(zrow, *row[1:])
        from_z1, from_row, from_z3 = zrow[1], row[2][1:], zrow[2]
        if attended is not None:
            from_z1, from_row, from_z3 = (behind(x, attended) for x in (from_z1, from_row, from_z3))
        prior = (across(from_z1, 1), ahead(from_row), across(from_z3, 3))
        first, turn = zrow, (prior[0], prior[2])
        outs = attend(col, start_flat, start_wide, row, zrow, prior)
        attended = outs[0]
        pieces += [outs[0]] + [across(outs[r], r) for r in (1, 2, 3)]
        late.append(z_late)
        zrows.append(zrow)
    late = [ahead(behind(x, zrows[1])) for x in late]
    mixed = unpack(col, pieces)
    kv = cache(col, slots, zrows[0], late[0], zrows[1], late[1])
    return (mixed, kv)


def solution(mesh):
    in_specs = (
        P(("req", "blk"), "head"),
        P(("req", "blk"), "head"),
        P(("req", "blk"), "head"),
        P(("req", "blk")),
        P(("req", "blk")),
    )
    out_specs = (P(("req", "blk"), "head"), P(("req", "blk"), None, None, "head"))
    return jax.shard_map(
        per_device, mesh=mesh, in_specs=in_specs, out_specs=out_specs, check_vma=False
    )
```
